32 devices in a mesh: section: 4 (over y, x), expert: 8 (over z, core).
Axes of the slice: x: 2, y: 2, z: 4, core: 2. Of those that a mesh axis runs over, the one named last changes fastest.
Arguments:
- tokens: bfloat16 [2, 256, 7168], P(None, 'expert'), may hold values from -6 to 6
- norm_gain: float32 [4, 7168], P('section'), may hold values from 0.25 to 1.75
- w_gate: bfloat16 [4, 7168, 2048], P('section', None, 'expert'), may hold values from -0.0625 to 0.0625
- w_up: bfloat16 [4, 7168, 2048], P('section', None, 'expert'), may hold values from -0.0625 to 0.0625
- w_down: bfloat16 [4, 2048, 7168], P('section', 'expert'), may hold values from -0.1875 to 0.1875
- expert_ids: int32 [4, 2, 256, 1], P('section', None, 'expert'), may hold values from 0 to 1; in each aligned block of 32 rows (0 to 31, 32 to 63, ..., all dimensions but the last counted through in order) at most 24 rows name the same one
- gate_weight: float32 [4, 2, 256, 1], P('section', None, 'expert'), may hold values from 0.3 to 1.5
- capacity: int32 [4, 2], P('section'), may hold values from 64 to 192
Outputs:
- results: bfloat16 [2, 256, 7168], P(None, 'expert', 'section')
The draws below stay inside these ranges and needn't reach their ends.
Inputs may be any that keep to these rules, and one draw needn't show every extreme that they name: `expert_ids`: A token's 1 expert differ. In each aligned block of 32 tokens (the tokens of one device in one span and layer) no expert is named by more than 24 tokens, a bound that some block reaches.
All inputs are finite; a program needn't handle non-finite values.
Results may differ from the reference program's by a relative error of at most 0.0095.
Values may be sent and summed in bfloat16 or wider, within the bound.
No kernel may reach another device: no remote copies, remote signals or barrier semaphores. Data moves between devices by JAX's collectives and lax.ppermute only.
A program may use at most 128 MiB of HBM per device.

```python
import math
import jax
import jax.numpy as jnp
import numpy as np
from jax import lax

D = 7168
FF = 1024
SPLIT = 4
TOPK = 1
TOK_DEV = 32
SPANS = 2
EH_DEV = 256
EXPERTS = 2
SLOTS = 24
SPAN_TOK = 256
N_SECTION = 4


def set_ends(entries, rng, least, high):
    index_at = [jax.random.randint(jax.random.fold_in(rng, axis), (), 0, length) for axis, length in enumerate(entries.shape)]
    widest = entries.shape.index(max(entries.shape))
    beside = index_at[:widest] + [(index_at[widest] + 1) % entries.shape[widest]] + index_at[widest + 1:]
    return entries.at[tuple(index_at)].set(least).at[tuple(beside)].set(high)


def level_of(own_key, shape, split, least, largest):
    loudness = 1.0
    for dim, parts in split:
        steps = jax.random.uniform(jax.random.fold_in(jax.random.fold_in(own_key, 6), dim), (parts,), jnp.float32, least / len(split), largest / len(split))
        loudness = loudness * jnp.repeat(jnp.exp(steps), shape[dim] // parts).reshape((-1,) + (1,) * (len(shape) - 1 - dim))
    return loudness


def shared_out(own_key, own, number, rows, count, top, most, lean):
    ranking = jax.random.permutation(own_key, count)
    heavy_load, common = portions_of(count, rows * top, most, lean, True), portions_of(count, rows * top, most, lean, False)
    places = jnp.arange(count)

    def named(tallies, offset_by):
        used = int((tallies > 0).sum())
        fixed = max(1, used // 4)
        passed = fixed + (places - fixed + offset_by * (used - fixed)) % max(1, count - fixed)
        return jnp.zeros((count,), jnp.int32).at[ranking[jnp.where(places < fixed, places, passed)]].set(jnp.asarray(tallies, jnp.int32))

    tallies = jnp.where(number % 4 == 0, named(heavy_load, number // 4), named(common, number - number // 4 - 1))
    mixed = jax.random.permutation(jax.random.fold_in(own, 3), count)
    giver, taker = mixed[0:count // 2 * 2:2], mixed[1:count // 2 * 2:2]
    slack = jnp.minimum(tallies[giver] - 1, most - tallies[taker]) // 2
    slack = jnp.where((giver == ranking[0]) | (taker == ranking[0]) | (tallies[taker] == 0), 0, jnp.maximum(slack, 0))
    passed = jax.random.randint(jax.random.fold_in(own, 4), (count // 2,), 0, 1 << 20) % (slack + 1)
    tallies = tallies.at[giver].add(-passed).at[taker].add(passed)
    members = jnp.searchsorted(jnp.cumsum(tallies), jnp.arange(rows * top), side="right").astype(jnp.int32)
    grid = members.reshape(top, rows).T
    grid = grid[jax.random.permutation(jax.random.fold_in(own, 1), rows)]
    offset_by = jax.random.randint(jax.random.fold_in(own, 2), (rows, 1), 0, top)
    return jnp.take_along_axis(grid, (jnp.arange(top)[None, :] + offset_by) % top, axis=1)


def portions_of(count, total, limit, lean, full):
    loads = [(1 << 20) // math.isqrt(rank ** lean) + 1 for rank in range(1, count + 1)]
    largest = limit if full else min(limit, max(-(-total // count), total * loads[0] // sum(loads)))
    least = 1 if total - largest >= count - 1 else 0
    holding, spare = [largest] + [least] * (count - 1), total - largest - least * (count - 1)
    while spare > 0:
        candidates = [i for i in range(1, count) if holding[i] < largest] or [i for i in range(1, count) if holding[i] < limit]
        pool, budget = sum([loads[i] for i in candidates]), spare
        for i in candidates:
            addition = min(limit - holding[i], max(1, budget * loads[i] // pool), spare)
            holding[i] = holding[i] + addition
            spare = spare - addition
    return np.array(holding)


def centred(key, dims, width, bound, pieces=(), held_as=jnp.bfloat16):
    result = width * jax.random.normal(key, dims, jnp.float32)
    if pieces:
        result = result * level_of(key, dims, pieces, -0.22, 0.18)
    return jnp.clip(result, -bound, bound).astype(held_as)


def setup_inputs(seed: int = 0) -> dict:
    key_of = jax.random.split(jax.random.key(seed), 9)
    tokens = centred(key_of[0], (SPANS, SPAN_TOK, D), 1.0, 6.0, ((1, 8),))
    norm_gain = jnp.clip(1.0 + 0.15 * jax.random.normal(key_of[1], (N_SECTION, D), jnp.float32), 0.25, 1.75)
    w_gate = centred(key_of[2], (N_SECTION, D, EXPERTS * FF), D ** -0.5, 0.0625, ((0, 4), (2, 8)))
    w_up = centred(key_of[3], (N_SECTION, D, EXPERTS * FF), D ** -0.5, 0.0625, ((0, 4), (2, 8)))
    w_down = centred(key_of[4], (N_SECTION, EXPERTS * FF, D), FF ** -0.5, 0.1875, ((0, 4), (1, 8)))
    expert_ids_keys = jax.random.split(jax.random.fold_in(key_of[5], 1), N_SECTION * SPANS * SPAN_TOK // TOK_DEV)
    expert_ids_turns = jax.random.permutation(jax.random.fold_in(key_of[5], 3), N_SECTION * SPANS * SPAN_TOK // TOK_DEV)
    expert_ids = jax.vmap(lambda own, number: shared_out(jax.random.fold_in(key_of[5], 2), own, number, TOK_DEV, EXPERTS, TOPK, SLOTS, 2))(expert_ids_keys, expert_ids_turns).reshape((N_SECTION, SPANS, SPAN_TOK, TOPK))
    gate_weight = jnp.clip(0.3 + 1.2 * jax.random.uniform(key_of[6], (N_SECTION, SPANS, SPAN_TOK, TOPK), jnp.float32) ** level_of(key_of[6], (N_SECTION, SPANS, SPAN_TOK, TOPK), ((0, 4), (2, 8)), -0.2, 0.2), 0.3, 1.5)
    capacity = set_ends(jax.random.randint(key_of[7], (N_SECTION, EXPERTS), SPAN_TOK * TOPK // (2 * EXPERTS), 3 * SPAN_TOK * TOPK // (2 * EXPERTS) + 1), jax.random.fold_in(key_of[7], 1), SPAN_TOK * TOPK // (2 * EXPERTS), (3 * SPAN_TOK * TOPK // (2 * EXPERTS) + 1) - 1).astype(jnp.int32)
    return dict(tokens=tokens, norm_gain=norm_gain, w_gate=w_gate, w_up=w_up, w_down=w_down, expert_ids=expert_ids, gate_weight=gate_weight, capacity=capacity)


def moe_layer(stream, gain, gate_full, up_full, down_full, routed_ids, gate_values, limits):
    span_rows = stream.shape[0]
    blocks = span_rows // TOK_DEV
    assigned = TOK_DEV * TOPK
    widened = stream.astype(jnp.float32)
    stats = lax.optimization_barrier(jnp.mean(widened * widened, axis=-1, keepdims=True))
    normed = (widened * lax.rsqrt(stats + 1e-06) * gain[None, :]).astype(jnp.bfloat16)
    flat_ids = routed_ids.reshape(blocks, assigned).astype(jnp.int32)
    order = jnp.arange(assigned, dtype=jnp.int32)
    earlier = order[:, None] > order[None, :]
    alike = flat_ids[:, :, None] == flat_ids[:, None, :]
    slots = lax.optimization_barrier(jnp.sum((alike & earlier[None]).astype(jnp.int32), axis=-1))
    expert_iota = jnp.arange(EXPERTS, dtype=jnp.int32)
    counts = lax.optimization_barrier(jnp.sum((flat_ids[:, :, None] == expert_iota[None, None, :]).astype(jnp.int32), axis=1))
    before = jnp.cumsum(counts, axis=0) - counts
    queue = jnp.take_along_axis(before, flat_ids, axis=1) + slots
    keep = queue < limits[flat_ids]
    position = (jnp.arange(blocks, dtype=jnp.int32)[:, None] * SLOTS + slots).astype(jnp.int32)
    rows = jnp.repeat(normed.reshape(blocks, TOK_DEV, D), TOPK, axis=1).reshape(-1, D)
    buffers = jnp.zeros((EXPERTS, blocks * SLOTS, D), jnp.bfloat16)
    buffers = buffers.at[flat_ids.reshape(-1), position.reshape(-1)].set(rows)

    def one_expert(expert):
        expert_rows = lax.dynamic_index_in_dim(buffers, expert, 0, keepdims=False)
        total = jnp.zeros((blocks * SLOTS, D), jnp.float32)
        for piece in range(SPLIT):
            column = (expert * FF + piece * EH_DEV).astype(jnp.int32)
            gate_cols = lax.dynamic_slice_in_dim(gate_full, column, EH_DEV, 1)
            up_cols = lax.dynamic_slice_in_dim(up_full, column, EH_DEV, 1)
            down_rows = lax.dynamic_slice_in_dim(down_full, column, EH_DEV, 0)
            gate_out = jnp.dot(expert_rows, gate_cols, preferred_element_type=jnp.float32)
            up_out = jnp.dot(expert_rows, up_cols, preferred_element_type=jnp.float32)
            hidden = (jax.nn.silu(gate_out) * up_out).astype(jnp.bfloat16)
            partial_out = jnp.dot(hidden, down_rows, preferred_element_type=jnp.float32).astype(jnp.bfloat16)
            partial_out = lax.optimization_barrier(partial_out)
            total = total + partial_out.astype(jnp.float32)
        return total
    outputs = lax.map(one_expert, jnp.arange(EXPERTS, dtype=jnp.int32))
    picked = outputs[flat_ids.reshape(-1), position.reshape(-1)]
    weights = jnp.where(keep.reshape(-1), gate_values.reshape(-1).astype(jnp.float32), jnp.float32(0.0))
    moe_out = lax.optimization_barrier(jnp.sum((picked * weights[:, None]).reshape(span_rows, TOPK, D), axis=1))
    return (widened + moe_out).astype(jnp.bfloat16)

def reference(tokens, norm_gain, w_gate, w_up, w_down, expert_ids, gate_weight, capacity):
    finals = []
    for span in range(SPANS):
        stream = tokens[span]
        for layer_index in range(N_SECTION):
            stream = moe_layer(stream, norm_gain[layer_index], w_gate[layer_index], w_up[layer_index], w_down[layer_index], expert_ids[layer_index, span], gate_weight[layer_index, span], capacity[layer_index])
        finals.append(stream)
    return jnp.stack(finals)
```

```python
import functools

import jax
import jax.numpy as jnp
from jax import lax
from jax.experimental import pallas as pl
from jax.experimental.pallas import tpu as pltpu
from jax.sharding import PartitionSpec as P

EPSILON = 1e-06


def entering(array, axis, combine, identity):
    length, place = (lax.axis_size(axis), lax.axis_index(axis))
    everything = lax.all_gather(array, axis)
    start = jnp.broadcast_to(jnp.asarray(identity, array.dtype), array.shape)

    def hop(k, before):
        reached = k < place
        new = combine(before, everything[k])
        return jnp.where(reached, new, before)

    return lax.fori_loop(0, length, hop, start)


def shifted(array, axis, by):
    length = lax.axis_size(axis)
    pairs = [(i, i + by) for i in range(length) if 0 <= i + by < length]
    return lax.ppermute(array, axis, pairs)


def slot_numbers(routed):
    length = routed.shape[-1]
    order = jnp.arange(length, dtype=jnp.int32)
    earlier = order[:, None] > order[None, :]
    alike = routed[..., :, None] == routed[..., None, :]
    return jnp.sum((alike & earlier).astype(jnp.int32), axis=-1)


def add_counts(earlier_counts, later_counts):
    return earlier_counts + later_counts


def expert_rows(arrived, gate_cols, up_cols, down_rows):
    width = arrived.shape[-1]
    flat_rows = arrived.reshape(-1, width)
    gate_out = jnp.dot(flat_rows, gate_cols, preferred_element_type=jnp.float32)
    up_out = jnp.dot(flat_rows, up_cols, preferred_element_type=jnp.float32)
    hidden = (jax.nn.silu(gate_out) * up_out).astype(jnp.bfloat16)
    partial_out = jnp.dot(hidden, down_rows, preferred_element_type=jnp.float32).astype(
        jnp.bfloat16
    )
    return partial_out.reshape(arrived.shape)


def moe_layer(
    stream, gain, gate_cols, up_cols, down_rows, routed_ids, gate_values, limits, slot_count
):
    token_rows, width = stream.shape
    top_count = routed_ids.shape[-1]
    expert_total = limits.shape[0]
    device_count = lax.axis_size("expert")
    split_count = device_count // expert_total
    widened = stream.astype(jnp.float32)
    stats = jnp.mean(widened * widened, axis=-1, keepdims=True)
    normed = (widened * lax.rsqrt(stats + EPSILON) * gain[None, :]).astype(jnp.bfloat16)
    flat_ids = routed_ids.reshape(-1)
    slots = slot_numbers(flat_ids)
    expert_iota = jnp.arange(expert_total, dtype=jnp.int32)
    onehot_ids = (flat_ids[:, None] == expert_iota[None, :]).astype(jnp.int32)
    counts = jnp.sum(onehot_ids, axis=0)
    before = entering(counts, "expert", add_counts, jnp.zeros_like(counts))
    queue = jnp.sum(onehot_ids * before[None, :], axis=1) + slots
    bound = jnp.sum(onehot_ids * limits[None, :], axis=1)
    weights = jnp.where(queue < bound, gate_values.reshape(-1), jnp.float32(0.0))
    target = flat_ids * slot_count + slots
    buffer_iota = jnp.arange(expert_total * slot_count, dtype=jnp.int32)
    placed = (buffer_iota[None, :] == target[:, None]).astype(jnp.float32)
    select = jnp.sum(placed.reshape(token_rows, top_count, -1), axis=1).astype(jnp.bfloat16)
    packed = lax.dot_general(
        select, normed, (((0,), (0,)), ((), ())), preferred_element_type=jnp.float32
    ).astype(jnp.bfloat16)
    outgoing = jnp.repeat(packed.reshape(expert_total, slot_count, width), split_count, axis=0)
    partials = expert_rows(
        lax.all_to_all(outgoing, "expert", split_axis=0, concat_axis=0, tiled=True),
        gate_cols,
        up_cols,
        down_rows,
    )
    returned = lax.all_to_all(partials, "expert", split_axis=0, concat_axis=0, tiled=True)
    summed = jnp.sum(
        returned.reshape(expert_total, split_count, slot_count, width).astype(jnp.float32), axis=1
    ).reshape(-1, width)
    mixing = jnp.sum((placed * weights[:, None]).reshape(token_rows, top_count, -1), axis=1)
    moe_out = jnp.dot(
        mixing, summed, precision=lax.Precision.HIGHEST, preferred_element_type=jnp.float32
    )
    return (widened + moe_out).astype(jnp.bfloat16)


def relayed_body(tokens, norm_gain, w_gate, w_up, w_down, expert_ids, gate_weight, capacity):
    section_count = lax.axis_size("section")
    section_index = lax.axis_index("section")
    span_count, token_rows, width = tokens.shape
    top_count = expert_ids.shape[-1]
    expert_total = capacity.shape[-1]
    slot_count = min(token_rows, max(2, 3 * (token_rows * top_count) // (2 * expert_total)))
    held = jnp.zeros((token_rows, width), jnp.bfloat16)
    results = jnp.zeros((span_count, token_rows, width), jnp.bfloat16)
    moments = section_count + span_count - 1
    for moment in range(moments):
        position = moment - section_index
        active = (position >= 0) & (position < span_count)
        picked = jnp.clip(position, 0, span_count - 1)
        entry = tokens[min(moment, span_count - 1)]
        stream = jnp.where(section_index == 0, entry, held)
        routed = lax.dynamic_index_in_dim(expert_ids[0], picked, 0, keepdims=False)
        gates = lax.dynamic_index_in_dim(gate_weight[0], picked, 0, keepdims=False)
        layer_out = moe_layer(
            stream,
            norm_gain[0],
            w_gate[0],
            w_up[0],
            w_down[0],
            routed,
            gates,
            capacity[0],
            slot_count,
        )
        finished = active & (section_index == section_count - 1)
        results = jnp.where(
            finished, lax.dynamic_update_index_in_dim(results, layer_out, picked, 0), results
        )
        if moment + 1 < moments:
            held = shifted(layer_out, "section", 1)
    return lax.psum_scatter(
        results.astype(jnp.float32).astype(jnp.bfloat16), "section", scatter_dimension=2, tiled=True
    )


CORES = 2
LANES = 128
HOLDERS = ({0: 0, 1: 1, 2: 2}, {0: 0, 1: 1, 2: 2}, {1: 1, 2: 2, 3: 0}, {2: 2, 3: 0, 0: 1})


def flip_expert(array, by):
    count = lax.axis_size("expert")
    return lax.ppermute(array, "expert", [(e, e ^ by) for e in range(count)])


def send_sections(array, moves):
    count = lax.axis_size("expert")
    pairs = [(a * count + e, b * count + e) for a, b in moves for e in range(count)]
    return lax.ppermute(array, ("section", "expert"), pairs)


def hot_rows(slot_row, slots):
    tokens = slot_row.shape[-1]
    place = lax.broadcasted_iota(jnp.int32, (slots, tokens), 0)
    return (place == slot_row).astype(jnp.bfloat16)


def hot_cols(slot_col, slots):
    tokens = slot_col.shape[0]
    place = lax.broadcasted_iota(jnp.int32, (tokens, slots), 1)
    return (place == slot_col).astype(jnp.bfloat16)


def pack_kernel(slots, rows_ref, x_ref, own_out, other_out):
    for k, out in enumerate((own_out, other_out)):
        out[...] = jnp.dot(
            hot_rows(rows_ref[k : k + 1, :], slots), x_ref[...], preferred_element_type=jnp.float32
        ).astype(out.dtype)


def pack(x, rows, slots):
    piece = jax.ShapeDtypeStruct((slots, x.shape[-1]), x.dtype)
    vmem = pl.BlockSpec(memory_space=pltpu.VMEM)
    return pl.pallas_call(
        functools.partial(pack_kernel, slots),
        out_shape=(piece, piece),
        in_specs=[vmem] * 2,
        out_specs=(vmem, vmem),
        compiler_params=pltpu.CompilerParams(vmem_limit_bytes=8 << 20),
        name="pack",
    )(rows, x)


def combine_kernel(slots, last, columns, rows, weights, x_ref, own_ref, other_ref, *outs):
    dot = functools.partial(jnp.dot, preferred_element_type=jnp.float32)
    total = dot(hot_cols(columns[:, 0:1], slots), own_ref[...])
    total += dot(hot_cols(columns[:, 1:2], slots), other_ref[...])
    x = (x_ref[...].astype(jnp.float32) + weights[...] * total).astype(x_ref.dtype)
    outs[0][...] = x
    if not last:
        for k in range(2):
            outs[1 + k][...] = dot(hot_rows(rows[k : k + 1, :], slots), x).astype(x.dtype)


def combine(columns, rows, weights, x, own, other, slots, last):
    piece = jax.ShapeDtypeStruct((slots, x.shape[-1]), x.dtype)
    outs = (jax.ShapeDtypeStruct(x.shape, x.dtype),) + (() if last else (piece, piece))
    vmem = pl.BlockSpec(memory_space=pltpu.VMEM)
    return pl.pallas_call(
        functools.partial(combine_kernel, slots, last),
        out_shape=outs,
        in_specs=[vmem] * 6,
        out_specs=tuple(vmem for _ in outs),
        compiler_params=pltpu.CompilerParams(vmem_limit_bytes=8 << 20),
        name="combine",
    )(columns, rows, weights, x, own, other)


def expert_kernel(starts, part, width, cuts, at_ref, *refs):
    count = len(starts)
    inputs, gain = refs[:count], refs[count]
    own, away = refs[count + 1 : count + 4], refs[count + 4 : count + 7]
    outs = refs[count + 7 : count + 7 + len(cuts)]
    normed, sums, hidden, here_gate, here_up, here_down, arrivals = refs[count + 7 + len(cuts) :]
    here = (here_gate, here_up, here_down)
    dot = functools.partial(jnp.dot, preferred_element_type=jnp.float32)

    @pl.when(at_ref[0] == 1)
    def _():
        copies = [pltpu.make_async_copy(away[k], here[k], arrivals.at[k]) for k in range(3)]
        for copy in copies:
            copy.start()
        square = jnp.zeros((inputs[0].shape[0], 1), jnp.float32)
        fresh = [max(k * part - starts[k], 0) for k in range(count)]
        for k in range(count):
            row = inputs[k][:, fresh[k] :].astype(jnp.float32)
            square += jnp.sum(row * row, axis=-1, keepdims=True)
        scale = lax.rsqrt(square / width + EPSILON)
        for k in range(count):
            skip = fresh[k]
            row = inputs[k][:, skip:].astype(jnp.float32)
            row = row * scale * gain[:, starts[k] + skip : starts[k] + part]
            normed[k, :, skip:] = row.astype(normed.dtype)
            if skip:
                normed[k, :, :skip] = jnp.zeros((row.shape[0], skip), normed.dtype)

        def inward(slot, matrices):
            sums[...] = jnp.zeros_like(sums)

            def step(k, carry):
                start = pl.multiple_of(jnp.minimum(k * part, width - part), LANES)
                lhs = normed[k]
                for m, matrix in enumerate(matrices):
                    sums[m] += dot(lhs, matrix[pl.ds(start, part), :])
                return carry

            lax.fori_loop(0, count, step, 0)
            gate = sums[0]
            hidden[slot] = (gate / (1.0 + jnp.exp(-gate)) * sums[1]).astype(hidden.dtype)

        inward(0, own[:2])
        copies[0].wait()
        copies[1].wait()
        inward(1, here[:2])
        copies[2].wait()
        for (start, size), out in zip(cuts, outs):
            total = dot(hidden[0], own[2][:, start : start + size])
            total += dot(hidden[1], here[2][:, start : start + size])
            out[...] = total.astype(out.dtype)


def experts(at, pieces, gain, own, away, starts, cuts):
    count = len(starts)
    rows, part = pieces[0].shape
    width, units = own[0].shape
    vmem = pl.BlockSpec(memory_space=pltpu.VMEM)
    return pl.pallas_call(
        functools.partial(expert_kernel, starts, part, width, cuts),
        out_shape=tuple(jax.ShapeDtypeStruct((rows, size), jnp.bfloat16) for _, size in cuts),
        in_specs=[pl.BlockSpec(memory_space=pltpu.SMEM)]
        + [vmem] * (count + 4)
        + [pl.BlockSpec(memory_space=pl.ANY)] * 3,
        out_specs=tuple(vmem for _ in cuts),
        scratch_shapes=[
            pltpu.VMEM((count, rows, part), jnp.bfloat16),
            pltpu.VMEM((2, rows, units), jnp.float32),
            pltpu.VMEM((2, rows, units), jnp.bfloat16),
            pltpu.VMEM((width, units), jnp.bfloat16),
            pltpu.VMEM((width, units), jnp.bfloat16),
            pltpu.VMEM((units, width), jnp.bfloat16),
            pltpu.SemaphoreType.DMA((3,)),
        ],
        compiler_params=pltpu.CompilerParams(vmem_limit_bytes=24 << 20),
        cost_estimate=pl.CostEstimate(
            flops=12 * rows * units * width, bytes_accessed=6 * units * width, transcendentals=0
        ),
        name="experts",
    )(at, *pieces, gain, *own, *away)


def routing(expert_ids, gate_weight, capacity):
    section_count = lax.axis_size("section")
    place = lax.axis_index("expert")
    device_count = lax.axis_size("expert")
    expert_total = capacity.shape[-1]
    ids, gates = expert_ids[0, :, :, 0], gate_weight[0, :, :, 0]
    size = ids.size
    mine = jnp.concatenate(
        [ids.reshape(-1).astype(jnp.float32), gates.reshape(-1), capacity[0].astype(jnp.float32)]
    )
    mine = jnp.pad(mine, (0, -mine.size % LANES))
    every = lax.all_to_all(
        jnp.broadcast_to(mine, (section_count, mine.size)), "section", 0, 0, tiled=True
    )
    shape = (section_count,) + ids.shape
    all_ids = every[:, :size].reshape(shape).astype(jnp.int32)
    all_gates = every[:, size : 2 * size].reshape(shape)
    limits = every[:, 2 * size : 2 * size + expert_total].astype(jnp.int32)
    slots = slot_numbers(all_ids)
    group = place // (device_count // expert_total)
    is_mine = all_ids == group
    pairs = jnp.stack([jnp.where(is_mine, slots, -1), jnp.where(is_mine, -1, slots)], axis=2)
    iota = jnp.arange(expert_total, dtype=jnp.int32)
    onehot = (all_ids[..., None] == iota).astype(jnp.int32)
    counts = jnp.sum(onehot, axis=2).reshape(-1)
    counts = jnp.pad(counts, (0, -counts.size % LANES))
    arrived = lax.all_to_all(
        jnp.broadcast_to(counts, (device_count, counts.size)), "expert", 0, 0, tiled=True
    )
    lower = (jnp.arange(device_count, dtype=jnp.int32) < place)[:, None]
    before = jnp.sum(jnp.where(lower, arrived, 0), axis=0)
    before = before[: section_count * ids.shape[0] * expert_total]
    before = before.reshape(section_count, ids.shape[0], 1, expert_total)
    queue = jnp.sum(onehot * before, axis=-1) + slots
    bound = jnp.sum(onehot * limits[:, None, None, :], axis=-1)
    weights = jnp.where(queue < bound, all_gates, jnp.float32(0.0))
    return pairs, jnp.swapaxes(pairs, 2, 3), weights[..., None]


def by_section(values):
    section = lax.axis_index("section")
    return sum(jnp.where(section == s, v, 0) for s, v in values.items()).astype(jnp.int32)


def gathered(own, other):
    near = jnp.concatenate([own, flip_expert(other, 2 * CORES)], axis=0)
    return jnp.concatenate([near, flip_expert(near, CORES)], axis=0)


def given_back(rows):
    half = rows.shape[0] // 2
    near = rows[:half].astype(jnp.float32) + flip_expert(rows[half:], CORES).astype(jnp.float32)
    near = near.astype(rows.dtype)
    return near[: half // 2], flip_expert(near[half // 2 :], 2 * CORES)


def spread_body(tokens, norm_gain, w_gate, w_up, w_down, expert_ids, gate_weight, capacity):
    layers = lax.axis_size("section")
    section = lax.axis_index("section")
    span_count, token_rows, width = tokens.shape
    expert_total = capacity.shape[-1]
    slots = min(token_rows, max(2, 3 * token_rows // (2 * expert_total)))
    count = len(HOLDERS[0])
    part = -(-width // (count * LANES)) * LANES
    starts = tuple(min(k * part, width - part) for k in range(count))
    quarter = width // layers
    pairs, columns, weights = routing(expert_ids, gate_weight, capacity)
    own_weights = (w_gate[0], w_up[0], w_down[0])
    first = by_section({s: starts[k] for s, k in HOLDERS[0].items()})
    streams = []
    for c in range(span_count):
        x = lax.dynamic_slice_in_dim(tokens[c], first, part, 1)
        streams.append((x, *pack(x, pairs[0, c], slots)))
    away_weights = tuple(flip_expert(w, 1) for w in own_weights)
    for layer in range(layers):
        at = (section == layer).astype(jnp.int32).reshape(1)
        last = layer == layers - 1
        after = None if last else HOLDERS[layer + 1]
        cuts = tuple(
            (s * quarter, quarter) if last else (starts[s], part)
            for s in range(layers if last else count)
        )
        targets = {s: s for s in range(layers)} if last else after
        for c in range(span_count):
            x, own, other = streams[c]
            spread = gathered(own, other)
            pieces = [None] * count
            for s, k in HOLDERS[layer].items():
                pieces[k] = spread if s == layer else send_sections(spread, [(s, layer)])
            outs = experts(at, pieces, norm_gain, own_weights, away_weights, starts, cuts)
            sent = [
                send_sections(outs[k], [(layer, s)]) for s, k in targets.items() if s != layer
            ]
            rows = jnp.where(section == layer, outs[targets[layer]], sum(sent[1:], sent[0]))
            if last:
                x = final_share(x, starts, part, quarter)
            else:
                held = HOLDERS[layer]
                for s, k in after.items():
                    if held.get(s) != k:
                        source = next(a for a, b in held.items() if b == k)
                        x = jnp.where(section == s, send_sections(x, [(source, s)]), x)
            mine, others = given_back(rows)
            streams[c] = combine(
                columns[layer, c],
                pairs[min(layer + 1, layers - 1), c],
                weights[layer, c],
                x,
                mine,
                others,
                slots,
                last,
            )
    return jnp.stack([streams[c][0] for c in range(span_count)])


def final_share(x, starts, part, quarter):
    section = lax.axis_index("section")
    held = HOLDERS[-1]
    home = {k: s for s, k in held.items()}
    count, layers = len(starts), lax.axis_size("section")
    width = starts[-1] + part
    low = {s: min(s * quarter // part, count - 1) for s in range(layers)}
    high = {s: min(((s + 1) * quarter - 1) // part, count - 1) for s in range(layers)}

    def fetch(wanted):
        rounds = []
        for s, k in wanted.items():
            if home[k] == s:
                continue
            for moves in rounds:
                if all(home[k] != a and s != b for a, b in moves):
                    moves.append((home[k], s))
                    break
            else:
                rounds.append([(home[k], s)])
        result = x
        for moves in rounds:
            arrived = send_sections(x, moves)
            for _, s in moves:
                result = jnp.where(section == s, arrived, result)
        return result

    lower = fetch(low)
    upper = fetch({s: high[s] for s in range(layers) if high[s] != low[s]})
    skip = by_section({s: max(high[s] * part - starts[high[s]], 0) for s in range(layers)})
    upper = jnp.where(skip > 0, jnp.roll(upper, -(count * part - width), axis=1), upper)
    both = jnp.concatenate([lower, upper], axis=1)
    begin = by_section({s: s * quarter - starts[low[s]] for s in range(layers)})
    return lax.dynamic_slice_in_dim(both, begin, quarter, 1)


def solution(mesh):
    in_specs = (
        P(None, "expert", None),
        P("section", None),
        P("section", None, "expert"),
        P("section", None, "expert"),
        P("section", "expert", None),
        P("section", None, "expert", None),
        P("section", None, "expert", None),
        P("section", None),
    )
    out_specs = P(None, "expert", "section")

    def body(tokens, norm_gain, w_gate, w_up, w_down, expert_ids, gate_weight, capacity):
        shares, devices = mesh.shape["section"], mesh.shape["expert"]
        experts_here, top = capacity.shape[-1], expert_ids.shape[-1]
        fits = shares == 4 and experts_here == 2 and devices == CORES * 4 and top == 1
        plan = spread_body if fits else relayed_body
        return plan(
            tokens, norm_gain, w_gate, w_up, w_down, expert_ids, gate_weight, capacity
        )

    return jax.shard_map(body, mesh=mesh, in_specs=in_specs, out_specs=out_specs, check_vma=False)
```
